512 devices in a mesh: dp: 8 (over z_hi, x), space: 64 (over y, z_lo, core).
Axes of the slice: x: 4, y: 4, z: 16 (z_hi: 2, z_lo: 8; z = z_hi * 8 + z_lo), core: 2. Of those that a mesh axis runs over, the one named last changes fastest.
Arguments:
- queries: bfloat16 [8, 24576, 768], P('dp', 'space'), may hold values from -6 to 6, as said below
- keys: bfloat16 [8, 24576, 768], P('dp', 'space'), may hold values from -6 to 6, as said below
- values: bfloat16 [8, 24576, 768], P('dp', 'space'), may hold values from -6 to 6
- out_grad: bfloat16 [8, 24576, 768], P('dp', 'space'), may hold values from -6 to 6
- w_out: bfloat16 [768, 768], P('dp'), may hold values from -0.21875 to 0.21875
- neighbours: int32 [192, 9], P('space'), may hold values from 0 to 191, as said below
- live_count: int32 [192], P('space'), may hold values from 7 to 9
Outputs:
- query_grad: bfloat16 [8, 24576, 768], P('dp', 'space')
- key_grad: bfloat16 [8, 24576, 768], P('dp', 'space')
- value_grad: bfloat16 [8, 24576, 768], P('dp', 'space')
- weight_grad: float32 [768, 768], P('dp')
The draws below stay inside these ranges and needn't reach their ends.
Inputs may be any that keep to these rules, and one draw needn't show every extreme that they name: `queries`: mostly of order one. `keys`: mostly of order one. `neighbours`: slot 0 of block b is b itself; the slots of a row name distinct blocks, all held by the same tile as b or by the tiles one index lower or higher along space, cyclically. Slots from live_count on hold valid ids that are ignored.
All inputs are finite; a program needn't handle non-finite values.
Results may differ from the reference program's by a relative error of at most 0.022.
Values may be sent and summed in bfloat16 or wider, within the bound.
No kernel may reach another device: no remote copies, remote signals or barrier semaphores. Data moves between devices by JAX's collectives and lax.ppermute only.
A program may use at most 64 MiB of HBM per device.

```python
import math
import jax
import jax.numpy as jnp
from jax import lax

D = 768
HEADS = 12
HD = 64
BLK = 128
NB = 9
TOK_DEV = 384
MEMBERS = 8
TOKENS = 24576
NBLK = 192
N_SPACE = 64


def draw_queries(key, part):
    drawn_key = jax.random.fold_in(key, 11)
    base = jax.random.truncated_normal(drawn_key, -5.5, 5.5, (MEMBERS, TOKENS, D), jnp.float32)
    return base.astype(jnp.bfloat16)


def draw_keys(key, part):
    drawn_key = jax.random.fold_in(key, 12)
    base = jax.random.truncated_normal(drawn_key, -5.5, 5.5, (MEMBERS, TOKENS, D), jnp.float32)
    return base.astype(jnp.bfloat16)


def block_graph(key):
    graph_key = jax.random.fold_in(key, 7)
    nblock = TOK_DEV // BLK
    span = 3 * nblock

    def one(block):
        block_key = jax.random.fold_in(graph_key, block)
        local = block % nblock
        owner = block // nblock
        self_off = nblock + local
        cand = jax.random.permutation(block_key, span - 1).astype(jnp.int32)
        offsets = cand + (cand >= self_off).astype(jnp.int32)
        offsets = jnp.concatenate([jnp.reshape(self_off, (1,)).astype(jnp.int32), offsets[:NB - 1]])
        return jnp.mod((owner - 1) * nblock + offsets, NBLK).astype(jnp.int32)
    graph = jax.vmap(one)(jnp.arange(NBLK, dtype=jnp.int32))
    counts = jax.random.randint(jax.random.fold_in(graph_key, 9), (NBLK,), NB - 2, NB + 1).astype(jnp.int32)
    counts = counts.at[0].set(NB).at[1].set(NB - 2)
    return (graph, counts)


def draw_neighbours(key, part):
    return block_graph(key)[0]


def draw_live_count(key, part):
    return block_graph(key)[1]


def shard_levels(rng, extent, split, least, high):
    level, own = 1.0, jax.random.fold_in(rng, 6)
    for axis_at, blocks in split:
        draws = jnp.exp(jax.random.uniform(jax.random.fold_in(own, axis_at), (blocks,), jnp.float32, least / len(split), high / len(split)))
        level = level * jnp.repeat(draws, extent[axis_at] // blocks).reshape([-1 if axis == axis_at else 1 for axis in range(len(extent))])
    return level


def gaussian(rng, shape, width, limit, shards=(), kind=jnp.bfloat16):
    gain = shard_levels(rng, shape, shards, -0.22, 0.18) if shards else 1.0
    drawn = jax.random.normal(rng, shape, jnp.float32) * width * gain
    return jnp.minimum(jnp.maximum(drawn, -limit), limit).astype(kind)


def setup_inputs(seed: int = 0) -> dict:
    streams_of = jax.random.split(jax.random.key(seed), 8)
    queries = draw_queries(jax.random.fold_in(streams_of[7], 71), 0)
    keys = draw_keys(jax.random.fold_in(streams_of[7], 71), 0)
    values = gaussian(streams_of[2], (MEMBERS, TOKENS, D), 1.0, 6.0, ((0, 8), (1, 64)))
    out_grad = gaussian(streams_of[3], (MEMBERS, TOKENS, D), 1.0, 6.0, ((0, 8), (1, 64)))
    w_out = gaussian(streams_of[4], (D, D), D ** -0.5, 0.21875, ((0, 8),))
    neighbours = draw_neighbours(jax.random.fold_in(streams_of[7], 71), 0)
    live_count = draw_live_count(jax.random.fold_in(streams_of[7], 71), 0)
    return dict(queries=queries, keys=keys, values=values, out_grad=out_grad, w_out=w_out, neighbours=neighbours, live_count=live_count)


def block_terms(query_blk, d_blk, key_win, val_win, ids, live):
    scale = 1.0 / math.sqrt(HD)
    qh = query_blk.astype(jnp.float32).reshape(BLK, HEADS, HD)
    doh = d_blk.astype(jnp.float32).reshape(BLK, HEADS, HD)
    key_blk = key_win[ids].astype(jnp.float32).reshape(NB * BLK, HEADS, HD)
    val_blk = val_win[ids].astype(jnp.float32).reshape(NB * BLK, HEADS, HD)
    scores = jnp.einsum('qhd,khd->hqk', qh, key_blk) * scale
    keymask = jnp.repeat(jnp.arange(NB) < live, BLK)
    scores = jnp.where(keymask[None, None, :], scores, -1e+30)
    top = lax.optimization_barrier(jnp.max(scores, axis=-1, keepdims=True))
    expo = jnp.exp(scores - top)
    probs = expo / lax.optimization_barrier(jnp.sum(expo, axis=-1, keepdims=True))
    probs_half = lax.optimization_barrier(probs.astype(jnp.bfloat16)).astype(jnp.float32)
    attended = lax.optimization_barrier(jnp.einsum('hqk,khd->qhd', probs_half, val_blk).astype(jnp.bfloat16))
    delta = lax.optimization_barrier(jnp.sum(doh * attended.astype(jnp.float32), axis=-1))
    dprobs = jnp.einsum('qhd,khd->hqk', doh, val_blk)
    dscores = lax.optimization_barrier((probs * (dprobs - delta.T[:, :, None])).astype(jnp.bfloat16)).astype(jnp.float32)
    dquery = (jnp.einsum('hqk,khd->qhd', dscores, key_blk) * scale).astype(jnp.bfloat16)
    dkey = jnp.einsum('hqk,qhd->khd', dscores, qh) * scale
    dval = jnp.einsum('hqk,qhd->khd', probs_half, doh)
    return (attended.reshape(BLK, D), dquery.reshape(BLK, D), dkey.reshape(NB, BLK, D), dval.reshape(NB, BLK, D))

def member_pass(query_rows, key_rows, value_rows, grad_rows, w_out, neighbours, live_count):
    nblock = TOK_DEV // BLK
    d_attended = jnp.dot(grad_rows, w_out.T, preferred_element_type=jnp.float32).astype(jnp.bfloat16)
    key_blocks = key_rows.reshape(NBLK, BLK, D)
    val_blocks = value_rows.reshape(NBLK, BLK, D)

    def tile(index):
        win_ids = jnp.mod((index - 1) * nblock + jnp.arange(3 * nblock), NBLK).astype(jnp.int32)
        key_win = key_blocks[win_ids]
        val_win = val_blocks[win_ids]
        start = (index * nblock).astype(jnp.int32)
        ids_all = jnp.mod(lax.dynamic_slice_in_dim(neighbours, start, nblock, 0) - (index - 1) * nblock, NBLK).astype(jnp.int32)
        lives = lax.dynamic_slice_in_dim(live_count, start, nblock, 0)

        def one(carry, step):
            row = ((start + step) * BLK).astype(jnp.int32)
            query_blk = lax.dynamic_slice_in_dim(query_rows, row, BLK, 0)
            d_blk = lax.dynamic_slice_in_dim(d_attended, row, BLK, 0)
            ids = ids_all[step]
            attended, dquery, dkey, dval = block_terms(query_blk, d_blk, key_win, val_win, ids, lives[step])
            key_acc, val_acc = carry
            key_acc = key_acc.at[ids].add(dkey)
            val_acc = val_acc.at[ids].add(dval)
            return ((key_acc, val_acc), (attended, dquery))
        zeros = jnp.zeros((3 * nblock, BLK, D), jnp.float32)
        (key_acc, val_acc), (attended, dquery) = lax.scan(one, (zeros, zeros), jnp.arange(nblock))
        return (attended.reshape(TOK_DEV, D), dquery.reshape(TOK_DEV, D), key_acc, val_acc)
    attended, dquery, key_win_all, val_win_all = lax.map(tile, jnp.arange(N_SPACE))

    def combine(window):
        lower = lax.optimization_barrier(window[:, :nblock].astype(jnp.bfloat16)).astype(jnp.float32)
        own = window[:, nblock:2 * nblock]
        upper = lax.optimization_barrier(window[:, 2 * nblock:].astype(jnp.bfloat16)).astype(jnp.float32)
        total = own + jnp.roll(upper, 1, axis=0) + jnp.roll(lower, -1, axis=0)
        return total.astype(jnp.bfloat16).reshape(TOKENS, D)
    attended_all = attended.reshape(TOKENS, D)
    weight_term = lax.dot_general(attended_all, grad_rows, (((0,), (0,)), ((), ())), preferred_element_type=jnp.float32)
    return (dquery.reshape(TOKENS, D), combine(key_win_all), combine(val_win_all), weight_term)

def reference(queries, keys, values, out_grad, w_out, neighbours, live_count):

    def member(inputs):
        return member_pass(inputs[0], inputs[1], inputs[2], inputs[3], w_out, neighbours, live_count)
    query_grad, key_grad, value_grad, weight_terms = lax.map(member, (queries, keys, values, out_grad))
    return (query_grad, key_grad, value_grad, lax.optimization_barrier(jnp.sum(weight_terms, axis=0)))
```

```python
import jax
import jax.numpy as jnp
from jax import lax
from jax.experimental import pallas as pl
from jax.experimental.pallas import tpu as pltpu
from jax.sharding import PartitionSpec as P

HD = 64
BLK = 128
F32 = jnp.float32
BF = jnp.bfloat16
NT = (((1,), (1,)), ((), ()))
NN = (((1,), (0,)), ((), ()))


def mm(a, b, dims=NN):
    return lax.dot_general(a, b, dims, preferred_element_type=F32)


def heads_side(x, lane):
    zero = jnp.zeros_like(x)
    return jnp.concatenate([jnp.where(lane < HD, x, zero), jnp.where(lane < HD, zero, x)], axis=0)


def heads_rows(xt, row):
    zero = jnp.zeros_like(xt)
    return jnp.concatenate([jnp.where(row < HD, xt, zero), jnp.where(row < HD, zero, xt)], axis=1)


def fwd_kernel(bias_ref, q_ref, kb_ref, ko_ref, ka_ref, vb_ref, vo_ref, va_ref, og_ref,
               expo_ref, sum_ref, att_ref, wterm_ref, s_ref):
    tok = q_ref.shape[0]
    nblk = tok // BLK
    lane = lax.broadcasted_iota(jnp.int32, (tok, 2 * HD), 1)
    row = lax.broadcasted_iota(jnp.int32, (2 * HD, tok), 0)
    q = q_ref[...] * jnp.asarray(0.125, BF)
    qcat = heads_side(q, lane)
    top = None
    for t, k_ref in enumerate((kb_ref, ko_ref, ka_ref)):
        s = mm(k_ref[...], qcat, NT)
        for j in range(nblk):
            w = t * nblk + j
            part = s[j * BLK:(j + 1) * BLK] + bias_ref[w:w + 1, :]
            s_ref[w * BLK:(w + 1) * BLK, :] = part
            peak = jnp.max(part.reshape(BLK // 8, 8, 2 * tok), axis=0)
            top = peak if top is None else jnp.maximum(top, peak)
    top = jnp.max(top, axis=0, keepdims=True)
    total = jnp.zeros((8, 2 * tok), F32)
    acc = jnp.zeros((2 * HD, 2 * tok), F32)
    for t, v_ref in enumerate((vb_ref, vo_ref, va_ref)):
        e = jnp.exp(s_ref[t * tok:(t + 1) * tok, :] - top)
        total += jnp.sum(e.reshape(tok // 8, 8, 2 * tok), axis=0)
        eh = e.astype(BF)
        expo_ref[t * tok:(t + 1) * tok, :] = eh
        acc += mm(v_ref[...].T, eh)
    inv = 1.0 / jnp.sum(total, axis=0, keepdims=True)
    acc = acc * inv
    att = jnp.where(row < HD, acc[:, :tok], acc[:, tok:]).astype(BF)
    sum_ref[...] = inv
    att_ref[...] = att
    wterm_ref[...] = mm(att, og_ref[...]).astype(wterm_ref.dtype)


def bwd_kernel(q_ref, kb_ref, ko_ref, ka_ref, vb_ref, vo_ref, va_ref, og_ref, w_ref,
               expo_ref, sum_ref, att_ref,
               dq_ref, dkb_ref, dko_ref, dka_ref, dvb_ref, dvo_ref, dva_ref):
    tok = q_ref.shape[0]
    lane = lax.broadcasted_iota(jnp.int32, (tok, 2 * HD), 1)
    row = lax.broadcasted_iota(jnp.int32, (2 * HD, tok), 0)
    inv = sum_ref[...]
    qcat = heads_side(q_ref[...] * jnp.asarray(0.125, BF), lane)
    do_t = mm(w_ref[...], og_ref[...], NT).astype(BF)
    do_f = do_t.astype(F32)
    prod = do_f * att_ref[...].astype(F32)
    delta = jnp.concatenate([jnp.sum(prod[:HD], axis=0, keepdims=True),
                             jnp.sum(prod[HD:], axis=0, keepdims=True)], axis=1) * inv
    do_rows = (heads_rows(do_f, row) * inv).astype(BF)
    do_side = do_rows.T
    dq = jnp.zeros((2 * HD, 2 * tok), F32)
    for t, (k_ref, v_ref, dk_ref, dv_ref) in enumerate((
            (kb_ref, vb_ref, dkb_ref, dvb_ref), (ko_ref, vo_ref, dko_ref, dvo_ref),
            (ka_ref, va_ref, dka_ref, dva_ref))):
        eh = expo_ref[t * tok:(t + 1) * tok, :]
        dp = mm(v_ref[...], do_rows)
        ds = (eh.astype(F32) * (dp - delta)).astype(BF)
        dv_ref[...] = mm(eh, do_side).astype(dv_ref.dtype)
        dk_ref[...] = mm(ds, qcat).astype(dk_ref.dtype)
        dq += mm(k_ref[...].T, ds)
    dq = jnp.where(row < HD, dq[:, :tok], dq[:, tok:]) * 0.125
    dq_ref[...] = dq.T.astype(dq_ref.dtype)


def col(tok):
    return pl.BlockSpec((tok, 2 * HD), lambda p: (0, p))


def forward(bias, q, kb, ko, ka, vb, vo, va, og):
    tok, width = q.shape
    pairs = width // (2 * HD)
    c = col(tok)
    full = lambda a: pl.BlockSpec(a.shape, lambda p: (0, 0))
    return pl.pallas_call(
        fwd_kernel,
        grid=(pairs,),
        in_specs=[full(bias), c, c, c, c, c, c, c, full(og)],
        out_specs=[
            pl.BlockSpec((None, 3 * tok, 2 * tok), lambda p: (p, 0, 0)),
            pl.BlockSpec((None, 1, 2 * tok), lambda p: (p, 0, 0)),
            pl.BlockSpec((2 * HD, tok), lambda p: (p, 0)),
            pl.BlockSpec((2 * HD, width), lambda p: (p, 0)),
        ],
        out_shape=[
            jax.ShapeDtypeStruct((pairs, 3 * tok, 2 * tok), BF),
            jax.ShapeDtypeStruct((pairs, 1, 2 * tok), F32),
            jax.ShapeDtypeStruct((width, tok), BF),
            jax.ShapeDtypeStruct((width, width), BF),
        ],
        scratch_shapes=[pltpu.VMEM((3 * tok, 2 * tok), F32)],
        cost_estimate=pl.CostEstimate(flops=4 * 3 * tok * tok * width, bytes_accessed=16 << 20, transcendentals=3 * tok * tok * width // HD),
        name="fwd",
    )(bias, q, kb, ko, ka, vb, vo, va, og)


def backward(q, kb, ko, ka, vb, vo, va, og, w, expo, inv, att):
    tok, width = q.shape
    pairs = width // (2 * HD)
    c = col(tok)
    full = lambda a: pl.BlockSpec(a.shape, lambda p: (0, 0))
    half = jax.ShapeDtypeStruct((tok, width), BF)
    wide = jax.ShapeDtypeStruct((tok, width), F32)
    return pl.pallas_call(
        bwd_kernel,
        grid=(pairs,),
        in_specs=[c, c, c, c, c, c, c, full(og), pl.BlockSpec((2 * HD, width), lambda p: (p, 0)),
            pl.BlockSpec((None, 3 * tok, 2 * tok), lambda p: (p, 0, 0)),
            pl.BlockSpec((None, 1, 2 * tok), lambda p: (p, 0, 0)),
            pl.BlockSpec((2 * HD, tok), lambda p: (p, 0)),
        ],
        out_specs=[c] * 7,
        out_shape=[half, half, wide, half, half, wide, half],
        cost_estimate=pl.CostEstimate(flops=8 * 3 * tok * tok * width, bytes_accessed=20 << 20, transcendentals=0),
        name="bwd",
    )(q, kb, ko, ka, vb, vo, va, og, w, expo, inv, att)


def shifted(block, distance):
    count = lax.axis_size("space")
    return lax.ppermute(block, "space", [((i - distance) % count, i) for i in range(count)])


def block_bias(neighbours, live_count, tokens):
    nblock, slots = neighbours.shape
    total = nblock * lax.axis_size("space")
    ids = jnp.mod(neighbours - (lax.axis_index("space") - 1) * nblock, total)
    used = jnp.arange(slots)[None, :] < live_count[:, None]
    names = ids[None] == jnp.arange(3 * nblock)[:, None, None]
    live = jnp.any(names & used[None], axis=-1)
    bias = jnp.where(live, 0.0, -1e30).astype(F32)
    wide = jnp.broadcast_to(bias[:, None, :, None], (3 * nblock, 2, nblock, BLK))
    return wide.reshape(3 * nblock, 2 * tokens)


def body(queries, keys, values, out_grad, w_out, neighbours, live_count):
    q, k, v, og = queries[0], keys[0], values[0], out_grad[0]
    tokens, width = q.shape
    kb, ka = shifted(k, 1), shifted(k, -1)
    vb, va = shifted(v, 1), shifted(v, -1)
    w = lax.all_gather(w_out, "dp", axis=0, tiled=True)
    bias = block_bias(neighbours, live_count, tokens)
    expo, inv, att, wterm = forward(bias, q, kb, k, ka, vb, v, va, og)
    rows = width // lax.axis_size("dp")
    whole = lax.psum(wterm, ("dp", "space"))
    weight_grad = lax.dynamic_slice_in_dim(whole, lax.axis_index("dp") * rows, rows, 0).astype(F32)
    dq, dkb, dko, dka, dvb, dvo, dva = backward(q, kb, k, ka, vb, v, va, og, w, expo, inv, att)

    def total(own, upper, lower):
        return (own + shifted(upper, 1).astype(F32) + shifted(lower, -1).astype(F32)).astype(BF)

    dk = total(dko, dka, dkb)
    dv = total(dvo, dva, dvb)
    return (dq[None], dk[None], dv[None], weight_grad)


def solution(mesh):
    rows = P("dp", "space", None)
    return jax.shard_map(
        body,
        mesh=mesh,
        in_specs=(rows, rows, rows, rows, P("dp", None), P("space", None), P("space")),
        out_specs=(rows, rows, rows, P("dp", None)),
        check_vma=False,
    )
```

```python
import jax
import jax.numpy as jnp
from jax import lax
from jax.experimental import pallas as pl
from jax.experimental.pallas import tpu as pltpu
from jax.sharding import PartitionSpec as P

HD = 64
BLK = 128
F32 = jnp.float32
BF = jnp.bfloat16
NT = (((1,), (1,)), ((), ()))
NN = (((1,), (0,)), ((), ()))


def mm(a, b, dims=NN):
    return lax.dot_general(a, b, dims, preferred_element_type=F32)


def heads_side(x, lane):
    zero = jnp.zeros_like(x)
    return jnp.concatenate([jnp.where(lane < HD, x, zero), jnp.where(lane < HD, zero, x)], axis=0)


def heads_rows(xt, row):
    zero = jnp.zeros_like(xt)
    return jnp.concatenate([jnp.where(row < HD, xt, zero), jnp.where(row < HD, zero, xt)], axis=1)


def fwd_kernel(bias_ref, q_ref, kb_ref, ko_ref, ka_ref, vb_ref, vo_ref, va_ref, og_ref,
               expo_ref, sum_ref, att_ref, wterm_ref, s_ref):
    tok = q_ref.shape[0]
    nblk = tok // BLK
    lane = lax.broadcasted_iota(jnp.int32, (tok, 2 * HD), 1)
    row = lax.broadcasted_iota(jnp.int32, (2 * HD, tok), 0)
    q = q_ref[...] * jnp.asarray(0.125, BF)
    qcat = heads_side(q, lane)
    top = None
    for t, k_ref in enumerate((kb_ref, ko_ref, ka_ref)):
        s = mm(k_ref[...], qcat, NT)
        for j in range(nblk):
            w = t * nblk + j
            part = s[j * BLK:(j + 1) * BLK] + bias_ref[w:w + 1, :]
            s_ref[w * BLK:(w + 1) * BLK, :] = part
            peak = jnp.max(part.reshape(BLK // 8, 8, 2 * tok), axis=0)
            top = peak if top is None else jnp.maximum(top, peak)
    top = jnp.max(top, axis=0, keepdims=True)
    total = jnp.zeros((8, 2 * tok), F32)
    acc = jnp.zeros((2 * HD, 2 * tok), F32)
    for t, v_ref in enumerate((vb_ref, vo_ref, va_ref)):
        e = jnp.exp(s_ref[t * tok:(t + 1) * tok, :] - top)
        total += jnp.sum(e.reshape(tok // 8, 8, 2 * tok), axis=0)
        eh = e.astype(BF)
        expo_ref[t * tok:(t + 1) * tok, :] = eh
        acc += mm(v_ref[...].T, eh)
    inv = 1.0 / jnp.sum(total, axis=0, keepdims=True)
    acc = acc * inv
    att = jnp.where(row < HD, acc[:, :tok], acc[:, tok:]).astype(BF)
    sum_ref[...] = inv
    att_ref[...] = att
    wterm = mm(att, og_ref[...]).astype(wterm_ref.dtype)
    wide = wterm_ref.shape[2]
    wterm_ref[0] = wterm[:, :wide]
    wterm_ref[1] = wterm[:, wide:]


def bwd_kernel(place_ref, q_ref, kb_ref, ko_ref, ka_ref, vb_ref, vo_ref, va_ref, og_ref, w_ref, wx_ref,
               expo_ref, sum_ref, att_ref,
               dq_ref, dkb_ref, dko_ref, dka_ref, dvb_ref, dvo_ref, dva_ref, do_ref):
    tok = q_ref.shape[0]
    lane = lax.broadcasted_iota(jnp.int32, (tok, 2 * HD), 1)
    row = lax.broadcasted_iota(jnp.int32, (2 * HD, tok), 0)
    inv = sum_ref[...]
    qcat = heads_side(q_ref[...] * jnp.asarray(0.125, BF), lane)
    pair = pl.program_id(0)

    @pl.when(pair == 0)
    def _():
        shards = place_ref.shape[0] - 1
        rows = w_ref.shape[0] // shards
        wide = w_ref.shape[1]
        mine = place_ref[shards]
        og_mine = og_ref[:, pl.ds(pl.multiple_of(mine * wide, wide), wide)]
        og_other = og_ref[:, pl.ds(pl.multiple_of((1 - mine) * wide, wide), wide)]
        for r in range(shards):
            span = slice(r * rows, (r + 1) * rows)
            part = mm(w_ref[span, :], og_mine, NT) + mm(wx_ref[span, :], og_other, NT)
            do_ref[pl.ds(pl.multiple_of(place_ref[r] * rows, rows), rows), :] = part.astype(BF)

    do_t = do_ref[pl.ds(pl.multiple_of(pair * 2 * HD, 2 * HD), 2 * HD), :]
    do_f = do_t.astype(F32)
    prod = do_f * att_ref[...].astype(F32)
    delta = jnp.concatenate([jnp.sum(prod[:HD], axis=0, keepdims=True),
                             jnp.sum(prod[HD:], axis=0, keepdims=True)], axis=1) * inv
    do_rows = (heads_rows(do_f, row) * inv).astype(BF)
    do_side = do_rows.T
    dq = jnp.zeros((2 * HD, 2 * tok), F32)
    for t, (k_ref, v_ref, dk_ref, dv_ref) in enumerate((
            (kb_ref, vb_ref, dkb_ref, dvb_ref), (ko_ref, vo_ref, dko_ref, dvo_ref),
            (ka_ref, va_ref, dka_ref, dva_ref))):
        eh = expo_ref[t * tok:(t + 1) * tok, :]
        dp = mm(v_ref[...], do_rows)
        ds = (eh.astype(F32) * (dp - delta)).astype(BF)
        dv_ref[...] = mm(eh, do_side).astype(dv_ref.dtype)
        dk_ref[...] = mm(ds, qcat).astype(dk_ref.dtype)
        dq += mm(k_ref[...].T, ds)
    dq = jnp.where(row < HD, dq[:, :tok], dq[:, tok:]) * 0.125
    dq_ref[...] = dq.T.astype(dq_ref.dtype)


def col(tok):
    return pl.BlockSpec((tok, 2 * HD), lambda p: (0, p))


def forward(bias, q, kb, ko, ka, vb, vo, va, og):
    tok, width = q.shape
    pairs = width // (2 * HD)
    c = col(tok)
    full = lambda a: pl.BlockSpec(a.shape, lambda p: (0, 0))
    return pl.pallas_call(
        fwd_kernel,
        grid=(pairs,),
        in_specs=[full(bias), c, c, c, c, c, c, c, full(og)],
        out_specs=[
            pl.BlockSpec((None, 3 * tok, 2 * tok), lambda p: (p, 0, 0)),
            pl.BlockSpec((None, 1, 2 * tok), lambda p: (p, 0, 0)),
            pl.BlockSpec((2 * HD, tok), lambda p: (p, 0)),
            pl.BlockSpec((2, 2 * HD, width // 2), lambda p: (0, p, 0)),
        ],
        out_shape=[
            jax.ShapeDtypeStruct((pairs, 3 * tok, 2 * tok), BF),
            jax.ShapeDtypeStruct((pairs, 1, 2 * tok), F32),
            jax.ShapeDtypeStruct((width, tok), BF),
            jax.ShapeDtypeStruct((2, width, width // 2), BF),
        ],
        scratch_shapes=[pltpu.VMEM((3 * tok, 2 * tok), F32)],
        cost_estimate=pl.CostEstimate(flops=4 * 3 * tok * tok * width, bytes_accessed=16 << 20, transcendentals=3 * tok * tok * width // HD),
        name="fwd",
    )(bias, q, kb, ko, ka, vb, vo, va, og)


def backward(place, q, kb, ko, ka, vb, vo, va, og, w, wx, expo, inv, att):
    tok, width = q.shape
    pairs = width // (2 * HD)
    c = col(tok)
    full = lambda a: pl.BlockSpec(a.shape, lambda p: (0, 0))
    half = jax.ShapeDtypeStruct((tok, width), BF)
    wide = jax.ShapeDtypeStruct((tok, width), F32)
    return pl.pallas_call(
        bwd_kernel,
        grid=(pairs,),
        in_specs=[pl.BlockSpec(memory_space=pltpu.SMEM), c, c, c, c, c, c, c, full(og), full(w), full(wx),
            pl.BlockSpec((None, 3 * tok, 2 * tok), lambda p: (p, 0, 0)),
            pl.BlockSpec((None, 1, 2 * tok), lambda p: (p, 0, 0)),
            pl.BlockSpec((2 * HD, tok), lambda p: (p, 0)),
        ],
        out_specs=[c] * 7,
        out_shape=[half, half, wide, half, half, wide, half],
        scratch_shapes=[pltpu.VMEM((width, tok), BF)],
        cost_estimate=pl.CostEstimate(flops=8 * 3 * tok * tok * width, bytes_accessed=20 << 20, transcendentals=0),
        name="bwd",
    )(place, q, kb, ko, ka, vb, vo, va, og, w, wx, expo, inv, att)


def move(block, axis, target):
    return lax.ppermute(block, axis, [(i, target(i)) for i in range(lax.axis_size(axis))])


def shifted(block, distance):
    count = lax.axis_size("space")
    return move(block, "space", lambda i: (i + distance) % count)


def core_swap(block):
    return move(block, "space", lambda i: i ^ 1)


def along_y(block, distance):
    return move(block, "space", lambda i: (i & 15) | ((((i >> 4) + distance) & 3) << 4))


def along_x(block, distance):
    return move(block, "dp", lambda i: (i & 4) | ((i + distance) & 3))


def far_swap(block):
    return move(block, "dp", lambda i: i ^ 4)


def add_up(*terms):
    total = terms[0].astype(F32)
    for term in terms[1:]:
        total = total + term.astype(F32)
    return lax.optimization_barrier(total.astype(BF))


def pick(array, index, axis):
    return lax.dynamic_index_in_dim(array, index, axis, keepdims=False)


def gather_weight(w_out):
    dp, space = lax.axis_index("dp"), lax.axis_index("space")
    half = w_out.shape[1] // 2
    near = lax.dynamic_slice_in_dim(w_out, (space & 1) * half, half, 1)
    far = far_swap(near)
    blocks = [near, *(along_x(near, d) for d in (1, 2, 3)), far, *(along_x(far, d) for d in (1, 2, 3))]
    mine = jnp.concatenate(blocks, axis=0)
    places = [((dp & 4) ^ (4 * f)) | ((dp - d) & 3) for f in (0, 1) for d in range(4)]
    return mine, core_swap(mine), jnp.stack([*places, space & 1]).astype(jnp.int32)


def sum_weight(wterm):
    dp, space = lax.axis_index("dp"), lax.axis_index("space")
    far, x, y, core = dp >> 2, dp & 3, space >> 4, space & 1
    rows, half = wterm.shape[1] // 8, wterm.shape[2]
    part = add_up(pick(wterm, core, 0), core_swap(pick(wterm, 1 - core, 0)))
    part = part.reshape(2, 4, rows, half)
    part = add_up(pick(part, x, 1), *(along_x(pick(part, (x + d) & 3, 1), d) for d in (1, 2, 3)))
    part = part.reshape(2, 4, rows // 4, half)
    part = add_up(pick(part, y, 1), *(along_y(pick(part, (y + d) & 3, 1), d) for d in (1, 2, 3)))
    part = add_up(pick(part, far, 0), far_swap(pick(part, 1 - far, 0)))
    for bit in (2, 4, 8):
        part = add_up(part, move(part, "space", lambda i: i ^ bit))
    ring = jnp.stack([part, *(along_y(part, d) for d in (3, 2, 1))])
    ring = jnp.concatenate([ring, ring], axis=0)
    mine = lax.dynamic_slice_in_dim(ring, (-y) & 3, 4, 0).reshape(rows, half)
    other = core_swap(mine)
    pair = jnp.where(core == 0, jnp.concatenate([mine, other], axis=1), jnp.concatenate([other, mine], axis=1))
    return pair.astype(F32)


def block_bias(neighbours, live_count, tokens):
    nblock, slots = neighbours.shape
    total = nblock * lax.axis_size("space")
    ids = jnp.mod(neighbours - (lax.axis_index("space") - 1) * nblock, total)
    used = jnp.arange(slots)[None, :] < live_count[:, None]
    names = ids[None] == jnp.arange(3 * nblock)[:, None, None]
    live = jnp.any(names & used[None], axis=-1)
    bias = jnp.where(live, 0.0, -1e30).astype(F32)
    wide = jnp.broadcast_to(bias[:, None, :, None], (3 * nblock, 2, nblock, BLK))
    return wide.reshape(3 * nblock, 2 * tokens)


def body(queries, keys, values, out_grad, w_out, neighbours, live_count):
    q, k, v, og = queries[0], keys[0], values[0], out_grad[0]
    tokens = q.shape[0]
    kb, ka = shifted(k, 1), shifted(k, -1)
    vb, va = shifted(v, 1), shifted(v, -1)
    w, wx, place = gather_weight(w_out)
    bias = block_bias(neighbours, live_count, tokens)
    expo, inv, att, wterm = forward(bias, q, kb, k, ka, vb, v, va, og)
    weight_grad = sum_weight(wterm)
    dq, dkb, dko, dka, dvb, dvo, dva = backward(place, q, kb, k, ka, vb, v, va, og, w, wx, expo, inv, att)

    def total(own, upper, lower):
        return (own + shifted(upper, 1).astype(F32) + shifted(lower, -1).astype(F32)).astype(BF)

    dk = total(dko, dka, dkb)
    dv = total(dvo, dva, dvb)
    return (dq[None], dk[None], dv[None], weight_grad)


def solution(mesh):
    rows = P("dp", "space", None)
    return jax.shard_map(
        body,
        mesh=mesh,
        in_specs=(rows, rows, rows, rows, P("dp", None), P("space", None), P("space")),
        out_specs=(rows, rows, rows, P("dp", None)),
        check_vma=False,
    )
```
